128 devices in a mesh: row: 8 (over x, y_lo), col: 16 (over z, y_hi, core).
Axes of the slice: x: 4, y: 4 (y_hi: 2, y_lo: 2; y = y_hi * 2 + y_lo), z: 4, core: 2. Of those that a mesh axis runs over, the one named last changes fastest.
Arguments:
- rhs: float32 [4, 8, 512, 2, 16, 512], P(None, 'row', None, None, 'col'), may hold values from -6 to 6, as said below
- panels: bfloat16 [2, 4, 8, 512, 1024], P(None, None, 'row', 'col'), may hold values from -6 to 6, as said below
- inverses: float32 [3, 512, 512], replicated, may hold values from -2 to 2, as said below
Outputs:
- new_rhs: float32 [4, 8, 512, 2, 16, 512], P(None, 'row', None, None, 'col')
- solved: float32 [2, 512, 512], P(None, 'row', 'col')
The draws below stay inside these ranges and needn't reach their ends.
Inputs may be any that keep to these rules, and one draw needn't show every extreme that they name: rhs is symmetric as a matrix of order 32 * 512. `panels`: A and E are upper triangular: panel rows of block n are zero in the first 512 columns, and the diagonal blocks (m,m) and (n,n) are upper triangular with positive diagonals. The inverses are upper triangular preconditioners, only near the true inverses, and are used as given.
All inputs are finite; a program needn't handle non-finite values.
Results may differ from the reference program's by a relative error of at most 0.0025.
Values may be sent and summed in bfloat16 or wider, within the bound.
No kernel may reach another device: no remote copies, remote signals or barrier semaphores. Data moves between devices by JAX's collectives and lax.ppermute only.
A program may use at most 128 MiB of HBM per device.

```python
import math
import jax
import jax.numpy as jnp
from jax import lax

B = 512
BCOL = 2
SWEEPS = 3
BLOCKS = 32
RB = 4


def diag_parts(key):
    seeds = jax.random.split(jax.random.fold_in(key, 7), 4)
    scale_a = jnp.exp(jax.random.uniform(seeds[0], (2, B), jnp.float32, 0.0, math.log(2.0)))
    ratio = jnp.exp(jax.random.uniform(seeds[1], (2, B), jnp.float32, math.log(0.8), math.log(1.25)))
    scale_e = scale_a * ratio
    strict = jnp.triu(jnp.ones((B, B), jnp.float32), 1)
    ident = jnp.eye(B, dtype=jnp.float32)
    upper_a = jax.random.normal(seeds[2], (2, B, B), jnp.float32) * (0.3 / math.sqrt(B)) * strict
    upper_e = jax.random.normal(seeds[3], (2, B, B), jnp.float32) * (0.3 / math.sqrt(B)) * strict
    blocks_a = scale_a[:, :, None] * (ident + upper_a)
    blocks_e = scale_e[:, :, None] * (ident + upper_e)
    noise_seeds = jax.random.split(jax.random.fold_in(key, 13), 4)
    diag_noise_a = jax.random.uniform(noise_seeds[0], (2, B), jnp.float32, -0.08, 0.08)
    diag_noise_e = jax.random.uniform(noise_seeds[1], (2, B), jnp.float32, -0.08, 0.08)
    extra_a = jnp.clip(jax.random.normal(noise_seeds[2], (2, B, B), jnp.float32), -6.0, 6.0) * (0.1 / math.sqrt(B)) * strict
    extra_e = jnp.clip(jax.random.normal(noise_seeds[3], (2, B, B), jnp.float32), -6.0, 6.0) * (0.1 / math.sqrt(B)) * strict
    approx_a = (ident * (1.0 + diag_noise_a[:, None, :]) - upper_a + extra_a) / scale_a[:, None, :]
    approximate_second_matrix = (ident * (1.0 + diag_noise_e[:, None, :]) - upper_e + extra_e) / scale_e[:, None, :]
    return (blocks_a, blocks_e, approx_a, approximate_second_matrix)


def draw_rhs(key, part):
    matrix_order = BLOCKS * B
    raw_values = jax.random.normal(key, (matrix_order, matrix_order), jnp.float32)
    symmetric = jnp.clip((raw_values + raw_values.T) * 0.7071, -6.0, 6.0)
    return symmetric.reshape(RB, BLOCKS // RB, B, BCOL, BLOCKS // BCOL, B)


def draw_panels(key, part):
    blocks_a, blocks_e, approx_a, approximate_second_matrix = diag_parts(key)
    dense_key = jax.random.fold_in(key, 11)
    matrix_order = BLOCKS * B
    dense = jnp.clip(jax.random.normal(dense_key, (2, matrix_order, 2 * B), jnp.float32), -6.0, 6.0)
    dense = dense * (1.0 / math.sqrt(B))
    last_start = matrix_order - B
    prev_start = last_start - B
    dense = dense.at[0, prev_start:last_start, :B].set(blocks_a[0])
    dense = dense.at[1, prev_start:last_start, :B].set(blocks_e[0])
    dense = dense.at[:, last_start:, :B].set(0.0)
    dense = dense.at[0, last_start:, B:].set(blocks_a[1])
    dense = dense.at[1, last_start:, B:].set(blocks_e[1])
    return dense.reshape(2, RB, BLOCKS // RB, B, 2 * B).astype(jnp.bfloat16)


def draw_inverses(key, part):
    blocks_a, blocks_e, approx_a, approximate_second_matrix = diag_parts(key)
    return jnp.stack([approx_a[0], approx_a[1], approximate_second_matrix[1]])


def setup_inputs(seed: int = 0) -> dict:
    splits = jax.random.split(jax.random.key(seed), 4)
    rhs = draw_rhs(jax.random.fold_in(splits[3], 71), 0)
    panels = draw_panels(jax.random.fold_in(splits[3], 71), 0)
    inverses = draw_inverses(jax.random.fold_in(splits[3], 71), 0)
    return {"rhs": rhs, "panels": panels, "inverses": inverses}


def product(left, right):
    return jnp.dot(left, right, precision=lax.Precision.HIGHEST, preferred_element_type=jnp.float32)


def reference(rhs, panels, inverses):
    matrix_order = BLOCKS * B
    matrix_rhs = rhs.reshape(matrix_order, matrix_order)
    panel_a = panels[0].reshape(matrix_order, 2 * B)
    panel_e = panels[1].reshape(matrix_order, 2 * B)
    last_start = matrix_order - B
    prev_start = last_start - B
    a_last = panel_a[last_start:, B:].astype(jnp.float32)
    e_last = panel_e[last_start:, B:].astype(jnp.float32)
    a_upper = panel_a[prev_start:last_start, B:].astype(jnp.float32)
    e_upper = panel_e[prev_start:last_start, B:].astype(jnp.float32)
    a_diag = panel_a[prev_start:last_start, :B].astype(jnp.float32)
    e_diag = panel_e[prev_start:last_start, :B].astype(jnp.float32)
    rhs_last = matrix_rhs[last_start:, last_start:]
    rhs_upper = matrix_rhs[prev_start:last_start, last_start:]
    diag_solution = jnp.zeros((B, B), jnp.float32)
    for sweep_index in range(SWEEPS):
        left_term = product(product(a_last, diag_solution), e_last.T)
        residual = -rhs_last - (left_term + left_term.T)
        update_term = product(product(inverses[1], residual), inverses[2].T)
        diag_solution = diag_solution + 0.25 * (update_term + update_term.T)
    target = -rhs_upper - (product(product(a_upper, diag_solution), e_last.T) + product(product(e_upper, diag_solution), a_last.T))
    next_solution = jnp.zeros((B, B), jnp.float32)
    for sweep_index in range(SWEEPS):
        residual = target - (product(product(a_diag, next_solution), e_last.T) + product(product(e_diag, next_solution), a_last.T))
        next_solution = next_solution + 0.5 * product(product(inverses[0], residual), inverses[2].T)
    solved = jnp.stack([diag_solution, next_solution])
    zero_block = jnp.zeros((B, B), jnp.float32)
    known_block = jnp.concatenate([jnp.concatenate([zero_block, next_solution], 1), jnp.concatenate([next_solution.T, diag_solution], 1)], 0).astype(jnp.bfloat16)
    z_panel = jnp.dot(panel_a, known_block, preferred_element_type=jnp.float32).astype(jnp.bfloat16)
    first_term = jnp.dot(z_panel, panel_e.T, preferred_element_type=jnp.float32)
    second_term = jnp.dot(panel_e, z_panel.T, preferred_element_type=jnp.float32)
    new_rhs = (matrix_rhs + first_term + second_term).reshape(rhs.shape)
    return new_rhs, solved
```

```python
import itertools

import jax
import jax.numpy as jnp
from jax import lax
from jax.experimental import pallas as pl
from jax.experimental.pallas import tpu as pltpu
from jax.sharding import PartitionSpec as P

SWEEPS = 3
AXES = ("row", "col")
BF = jnp.bfloat16
F32 = jnp.float32

ROOT = (3, 3, 3, 1)


def index(x, y, z, k):
    return (x * 2 + y % 2) * 16 + z * 4 + (y // 2) * 2 + k


def pairs(rule):
    out = []
    for x, y, z, k in itertools.product(range(4), range(4), range(4), range(2)):
        to = rule(x, y, z, k)
        if to is not None:
            out.append((index(x, y, z, k), index(*to)))
    return out


def send(value, rule):
    return lax.ppermute(value, AXES, pairs(rule))


def x_plus(x, y, z, k):
    return ((x + 1) % 4, y, z, k)


def x_minus(x, y, z, k):
    return ((x - 1) % 4, y, z, k)


def z_plus(x, y, z, k):
    return (x, y, (z + 1) % 4, k)


def z_minus(x, y, z, k):
    return (x, y, (z - 1) % 4, k)


def y_far(x, y, z, k):
    return (x, (y + 2) % 4, z, k)


def y_near(x, y, z, k):
    return (x, y ^ 1, z, k)


def core(x, y, z, k):
    return (x, y, z, 1 - k)


def broadcast_steps(order, source):
    steps = []
    done = []
    for axis in order:
        first = {}
        second = {}
        for at in itertools.product(range(4), repeat=3):
            free = [d for d in range(3) if d != axis and d not in done]
            if any(at[d] != source[d] for d in free):
                continue
            here = (at[axis] - source[axis]) % 4
            to = list(at)
            if here == 0:
                to[axis] = (at[axis] + 1) % 4
                first[at] = tuple(to)
                to[axis] = (at[axis] - 1) % 4
                second[at] = tuple(to)
            elif here == 1:
                to[axis] = (at[axis] + 1) % 4
                second[at] = tuple(to)
        steps += [first, second]
        done.append(axis)
    return steps


def broadcast(value, cuts):
    source = ROOT[:3]
    orders = ((0, 1, 2), (1, 2, 0), (2, 0, 1))
    chunks = [value[lo:hi] for lo, hi in zip(cuts[:-1], cuts[1:])]
    plans = [broadcast_steps(order, source) for order in orders]
    for step in range(6):
        got = [
            send(
                chunks[i],
                lambda x, y, z, k, i=i: (*plans[i][step][(x, y, z)], 1)
                if k == 1 and (x, y, z) in plans[i][step]
                else None,
            )
            for i in range(3)
        ]
        chunks = [chunks[i] + got[i] for i in range(3)]
    whole = jnp.concatenate(chunks, 0)
    other = send(whole, lambda x, y, z, k: (x, y, z, 0) if k == 1 else None)
    return whole + other


def gather_corner(piece, row_y):
    x0, z0 = ROOT[0], ROOT[2]
    got = send(
        piece,
        lambda x, y, z, k: (x, y, z, 1) if x == x0 and y % 2 == row_y and k == 0 else None,
    )
    both = jnp.stack([got, piece])
    far = send(
        both,
        lambda x, y, z, k: (x, y + 2, z, 1)
        if x == x0 and y % 2 == row_y and y < 2 and k == 1
        else None,
    )
    four = jnp.stack([far, both])
    out = []
    for z1 in range(4):
        if z1 == z0:
            out.append(four)
        else:
            out.append(
                send(
                    four,
                    lambda x, y, z, k, z1=z1: (x, y, z0, 1)
                    if x == x0 and y == 2 + row_y and z == z1 and k == 1
                    else None,
                )
            )
    return out


def dot(left, right):
    return jnp.dot(left, right, preferred_element_type=F32)


def dot_t(left, right):
    return lax.dot_general(left, right, (((1,), (1,)), ((), ())), preferred_element_type=F32)


def split(value, count):
    high = value.astype(BF)
    if count == 1:
        return [high]
    return [high, (value - high.astype(F32)).astype(BF)]


def terms(left, right):
    depth = max(len(left), len(right))
    return [(i, j) for i in range(len(left)) for j in range(len(right)) if i + j < depth]


def upper_times(upper, value):
    half = value[0].shape[0] // 2
    top = sum(dot(upper[i][:half, :], value[j]) for i, j in terms(upper, value))
    low = sum(dot(upper[i][half:, half:], value[j][half:, :]) for i, j in terms(upper, value))
    return jnp.concatenate([top, low], 0)


def times_upper_t(value, upper):
    half = value[0].shape[1] // 2
    left = sum(dot_t(value[i], upper[j][:half, :]) for i, j in terms(value, upper))
    right = sum(dot_t(value[i][:, half:], upper[j][half:, half:]) for i, j in terms(value, upper))
    return jnp.concatenate([left, right], 1)


def assemble(refs, part, lo, hi, out):
    step = refs[0].shape[3]
    at = 0
    for ref in refs:
        for yh in range(2):
            for k in range(2):
                out[at : at + step, :] = ref[yh, k, part, :, lo:hi]
                at += step


def last_kernel(flag, n0, n1, n2, n3, g, inv, x_out, xb_out, ae_out):
    @pl.when(flag[0] == 0)
    def _():
        xb_out[...] = jnp.zeros_like(xb_out)

    @pl.when(flag[0] == 1)
    def _():
        size = g.shape[0]
        for part in range(2):
            assemble((n0, n1, n2, n3), part, 0, size, ae_out.at[part])
        for sweep in range(SWEEPS):
            res = -g[...]
            if sweep:
                x = split(x_out[...], 2)
                left = times_upper_t(split(upper_times([ae_out[0]], x), 2), [ae_out[1]])
                res = res - (left + left.T)
            mid = split(upper_times(split(inv[1], 2), split(res, 2)), 2)
            upd = times_upper_t(mid, split(inv[2], 2))
            upd = 0.25 * (upd + upd.T)
            x_out[...] = x_out[...] + upd if sweep else upd
        xb_out[...] = x_out[...].astype(BF)


def upper_kernel(flag, m0, m1, m2, m3, g_t, inv, x_last, ae_last, xb_out, x, mm, rhs):
    @pl.when(flag[0] == 0)
    def _():
        xb_out[...] = jnp.zeros_like(xb_out)

    @pl.when(flag[0] == 1)
    def _():
        size = g_t.shape[0]
        for part in range(2):
            assemble((m0, m1, m2, m3), part, 0, 2 * size, mm.at[part])
        a_last, e_last = ae_last[0], ae_last[1]
        known = split(x_last[...], 2)
        left = sum(dot(mm[0, :, size:], v) for v in known)
        term = times_upper_t(split(left, 2), [e_last])
        left = sum(dot(mm[1, :, size:], v) for v in known)
        term = term + times_upper_t(split(left, 2), [a_last])
        rhs[...] = -g_t[...].T - term
        for sweep in range(SWEEPS):
            res = rhs[...]
            if sweep:
                v = split(x[...], 2)
                left = split(upper_times([mm[0, :, :size]], v), 2)
                term = times_upper_t(left, [e_last])
                left = split(upper_times([mm[1, :, :size]], v), 2)
                term = term + times_upper_t(left, [a_last])
                res = res - term
            mid = split(upper_times(split(inv[0], 2), split(res, 2)), 2)
            upd = 0.5 * times_upper_t(mid, split(inv[2], 2))
            x[...] = x[...] + upd if sweep else upd
        xb_out[...] = x[...].astype(BF)


VMEM = pl.BlockSpec(memory_space=pltpu.VMEM)
SMEM = pl.BlockSpec(memory_space=pltpu.SMEM)
LIMIT = 60 * 1024 * 1024


def solve_last(flag, pieces, g, inverses):
    size = g.shape[0]
    return pl.pallas_call(
        last_kernel,
        out_shape=(
            jax.ShapeDtypeStruct((size, size), F32),
            jax.ShapeDtypeStruct((size, size), BF),
            jax.ShapeDtypeStruct((2, size, size), BF),
        ),
        in_specs=[SMEM] + [VMEM] * 6,
        out_specs=(VMEM,) * 3,
        compiler_params=pltpu.CompilerParams(vmem_limit_bytes=LIMIT),
        cost_estimate=pl.CostEstimate(flops=9 * 10**9, bytes_accessed=8 * 10**6, transcendentals=0),
        name="solve_last",
    )(flag, *pieces, g, inverses)


def solve_upper(flag, pieces, g_t, inverses, x_last, ae_last):
    size = g_t.shape[0]
    return pl.pallas_call(
        upper_kernel,
        out_shape=jax.ShapeDtypeStruct((size, size), BF),
        in_specs=[SMEM] + [VMEM] * 8,
        out_specs=VMEM,
        scratch_shapes=[
            pltpu.VMEM((size, size), F32),
            pltpu.VMEM((2, size, 2 * size), BF),
            pltpu.VMEM((size, size), F32),
        ],
        compiler_params=pltpu.CompilerParams(vmem_limit_bytes=LIMIT),
        cost_estimate=pl.CostEstimate(flops=12 * 10**9, bytes_accessed=9 * 10**6, transcendentals=0),
        name="solve_upper",
    )(flag, *pieces, g_t, inverses, x_last, ae_last)


def update_kernel(at, rows, cols, x_last, x_upper, g, out, ye, za):
    size = x_last.shape[0]
    cut = cols.shape[3]
    lanes = g.shape[-1]
    chunks = 2 * size // lanes

    @pl.when(pl.program_id(0) == 0)
    def _():
        def piece(p, carry):
            row = lax.rem(at[0] + p // 2, 4) * 2 + (at[1] ^ lax.rem(p, 2))
            left = cols[p].reshape(4 * cut, 2 * size)
            low = dot_t(left[:, size:], x_upper[...]).astype(BF).reshape(2, 2, cut, size)
            high = dot(left[:, :size], x_upper[...]) + dot(left[:, size:], x_last[...])
            high = high.astype(BF).reshape(2, 2, cut, size)
            for b in range(2):
                place = pl.ds(pl.multiple_of(b * size + row * cut, cut), cut)
                za[place, :size] = low[0, b]
                za[place, size:] = high[0, b]
                ye[place, :size] = low[1, b]
                ye[place, size:] = high[1, b]
            return carry

        lax.fori_loop(0, cols.shape[0], piece, 0)

    wide = 2 * lanes
    step = rows.shape[5]
    tall = 4 * 4 * step

    def tile(j, carry):
        place = pl.ds(pl.multiple_of(j * wide, wide), wide)
        acc = dot_t(rows[0, :, :, 0].reshape(tall, 2 * size), ye[place, :])
        acc = acc + dot_t(rows[0, :, :, 1].reshape(tall, 2 * size), za[place, :])
        acc = acc.reshape(2, 2, 4, step, wide)
        for dk in range(2):
            k = at[4] ^ dk
            for dy in range(2):
                yh = at[3] ^ dy
                for a in range(4):
                    for part in range(2):
                        here = pl.ds(j * 2 + part, step, stride=chunks)
                        value = acc[dk, dy, a, :, part * lanes : (part + 1) * lanes]
                        out[a, 0, yh, k, here, :] = g[a, 0, yh, k, here, :] + value
        return carry

    lax.fori_loop(0, 2 * size // wide, tile, 0)


def update(at, rows, cols, x_last, x_upper, g):
    size = x_last.shape[0]
    block = (4, 1, 2, 2, g.shape[4], g.shape[5])
    spec = pl.BlockSpec(block, lambda i, at: (0, lax.rem(at[2] + i, 4), 0, 0, 0, 0))
    once = pl.Buffered(1)
    return pl.pallas_call(
        update_kernel,
        out_shape=jax.ShapeDtypeStruct(g.shape, F32),
        grid_spec=pltpu.PrefetchScalarGridSpec(
            num_scalar_prefetch=1,
            grid=(4,),
            in_specs=[
                pl.BlockSpec((1,) + rows.shape[1:], lambda i, at: (i,) + (0,) * 6),
                pl.BlockSpec(cols.shape, lambda i, at: (0,) * 5, pipeline_mode=once),
                pl.BlockSpec(x_last.shape, lambda i, at: (0, 0), pipeline_mode=once),
                pl.BlockSpec(x_upper.shape, lambda i, at: (0, 0), pipeline_mode=once),
                spec,
            ],
            out_specs=spec,
            scratch_shapes=[pltpu.VMEM((2 * size, 2 * size), BF)] * 2,
        ),
        compiler_params=pltpu.CompilerParams(
            dimension_semantics=("arbitrary",), vmem_limit_bytes=LIMIT
        ),
        cost_estimate=pl.CostEstimate(
            flops=12 * 10**9, bytes_accessed=30 * 10**6, transcendentals=0
        ),
        name="update",
    )(at, rows, cols, x_last, x_upper, g)


def gather_rows(local):
    far = send(local, y_far)
    own = jnp.stack([local, far])
    back = send(own, z_plus)
    front = send(own, z_minus)
    opposite = jnp.stack([send(back[0], z_plus), send(front[1], z_minus)])
    parts = [own, front, opposite, back]
    return jnp.stack([jnp.stack([p, send(p, core)]) for p in parts])


def gather_columns(local, upper_half):
    def rule(p):
        def to(x, y, z, k):
            row, col = x * 2 + y % 2, z * 4 + (y // 2) * 2 + k
            dest = row + 8 * (p ^ (col % 2))
            near, far = col // 2, dest
            return (near // 2, (far % 4) // 2 * 2 + near % 2, far // 4, far % 2)

        return to

    odd = lax.axis_index("col") % 2 == 1
    first, second = local[:, 0::2], local[:, 1::2]
    got0 = send(jnp.where(odd, second, first), rule(0))
    got1 = send(jnp.where(odd, first, second), rule(1))
    mine = jnp.concatenate(
        [jnp.where(upper_half, got1, got0), jnp.where(upper_half, got0, got1)], 2
    )
    own = jnp.stack([mine, send(mine, y_near)])
    back = send(own, x_plus)
    front = send(own, x_minus)
    opposite = jnp.stack([send(back[0], x_plus), send(front[1], x_minus)])
    return jnp.concatenate([own, front, opposite, back], 0)


def on_device(rhs, panels, inverses):
    row = lax.axis_index("row")
    col = lax.axis_index("col")
    size = rhs.shape[-1]
    blocks = panels.shape[1]
    local = panels[:, :, 0]
    g_here = rhs[blocks - 1, 0, :, rhs.shape[3] - 1, 0, :]
    root = index(*ROOT)
    flag = jnp.where(row * 16 + col == root, 1, 0).astype(jnp.int32)[None]

    last_rows = local[:, blocks - 1]
    n_pieces = gather_corner(last_rows[:, :, size:], 1)
    moved = send(last_rows, lambda x, y, z, k: (x, y + 1, z, k) if x == 3 and y % 2 == 0 else None)
    m_pieces = gather_corner(moved, 1)
    g_t = send(g_here, lambda x, y, z, k: ROOT if (x, y, z, k) == ROOT[:3] + (0,) else None)

    x_last, x_last_b, ae_last = solve_last(flag, n_pieces, g_here, inverses)
    x_upper_b = solve_upper(flag, m_pieces, g_t, inverses, x_last, ae_last)
    x_last_b = broadcast(x_last_b, (0, 176, 336, 512))
    x_upper_b = broadcast(x_upper_b, (0, 176, 336, 512))

    rows = gather_rows(local)
    cols = gather_columns(local, col >= 8)
    at = jnp.stack([row // 2, row % 2, col // 4, (col // 2) % 2, col % 2]).astype(jnp.int32)
    g = rhs.reshape(4, 4, 2, 2, 256, 128)
    new_rhs = update(at, rows, cols, x_last_b, x_upper_b, g).reshape(rhs.shape)

    rows_part = size // 8
    cols_part = size // 16
    both = jnp.stack([x_last_b, x_upper_b])
    solved = lax.dynamic_slice(
        both, (0, row * rows_part, col * cols_part), (2, rows_part, cols_part)
    ).astype(F32)
    return (new_rhs, solved)


def solution(mesh):
    in_specs = (P(None, "row", None, None, "col", None), P(None, None, "row", "col", None), P())
    out_specs = (P(None, "row", None, None, "col", None), P(None, "row", "col"))
    return jax.shard_map(
        on_device, mesh=mesh, in_specs=in_specs, out_specs=out_specs, check_vma=False
    )
```

```python
import itertools

import jax
import jax.numpy as jnp
from jax import lax
from jax.experimental import pallas as pl
from jax.experimental.pallas import tpu as pltpu
from jax.sharding import PartitionSpec as P


SWEEPS = 3
AXES = ("row", "col")
BF = jnp.bfloat16
F32 = jnp.float32

ROOT = (3, 3, 3, 1)


def index(x, y, z, k):
    return (x * 2 + y % 2) * 16 + z * 4 + (y // 2) * 2 + k


def pairs(rule):
    out = []
    for x, y, z, k in itertools.product(range(4), range(4), range(4), range(2)):
        to = rule(x, y, z, k)
        if to is not None:
            out.append((index(x, y, z, k), index(*to)))
    return out


def send(value, rule):
    return lax.ppermute(value, AXES, pairs(rule))


def x_plus(x, y, z, k):
    return ((x + 1) % 4, y, z, k)


def x_minus(x, y, z, k):
    return ((x - 1) % 4, y, z, k)


def y_far(x, y, z, k):
    return (x, (y + 2) % 4, z, k)


def y_near(x, y, z, k):
    return (x, y ^ 1, z, k)


def core(x, y, z, k):
    return (x, y, z, 1 - k)


def z_split(x, y, z, k):
    return (x, y, (z + (1 if k == 0 else -1)) % 4, k)


def z_far(x, y, z, k):
    return (x, y, (z + 2) % 4, k)


def broadcast(value):
    source = ROOT[:3]
    orders = ((1, 2, 0), (0, 1, 2))
    for step in range(3):
        got = []
        for shift in (2, 1, 3):

            def rule(x, y, z, k, shift=shift):
                at = [x, y, z]
                order = orders[k]
                if any(at[d] != source[d] for d in order[step:]):
                    return None
                at[order[step]] = (at[order[step]] + shift) % 4
                return (*at, k)

            got.append(send(value, rule))
        value = value + got[0] + got[1] + got[2]
    return value


def gather_corner(piece):
    x0, z0 = ROOT[0], ROOT[2]
    got = send(
        piece, lambda x, y, z, k: (x, y, z, 1) if x == x0 and y % 2 == 1 and k == 0 else None
    )
    both = jnp.stack([got, piece])
    far = send(both, lambda x, y, z, k: (x, 3, z, 1) if x == x0 and y == 1 and k == 1 else None)
    four = jnp.stack([far, both])
    size = piece.shape[-1] // 3
    out = []
    for part in (four[..., :size], four[..., size:]):
        pieces = [
            part
            if z1 == z0
            else send(
                part,
                lambda x, y, z, k, z1=z1: ROOT
                if x == x0 and y == 3 and z == z1 and k == 1
                else None,
            )
            for z1 in range(4)
        ]
        out.append(pieces)
    return out


def dot(left, right):
    return jnp.dot(left, right, preferred_element_type=F32)


def dot_t(left, right):
    return lax.dot_general(left, right, (((1,), (1,)), ((), ())), preferred_element_type=F32)


def split(value, count):
    high = value.astype(BF)
    if count == 1:
        return [high]
    return [high, (value - high.astype(F32)).astype(BF)]


def terms(left, right):
    depth = max(len(left), len(right))
    return [(i, j) for i in range(len(left)) for j in range(len(right)) if i + j < depth]


def upper_times(upper, value):
    half = value[0].shape[0] // 2
    top = sum(dot(upper[i][:half, :], value[j]) for i, j in terms(upper, value))
    low = sum(dot(upper[i][half:, half:], value[j][half:, :]) for i, j in terms(upper, value))
    return jnp.concatenate([top, low], 0)


def times_upper_t(value, upper):
    half = value[0].shape[1] // 2
    left = sum(dot_t(value[i], upper[j][:half, :]) for i, j in terms(value, upper))
    right = sum(dot_t(value[i][:, half:], upper[j][half:, half:]) for i, j in terms(value, upper))
    return jnp.concatenate([left, right], 1)


def assemble(refs, part, lo, hi, out):
    step = refs[0].shape[3]
    at = 0
    for ref in refs:
        for yh in range(2):
            for k in range(2):
                out[at : at + step, :] = ref[yh, k, part, :, lo:hi]
                at += step


def last_kernel(flag, n0, n1, n2, n3, g, inv, x_out, xb_out, ae_out, held, sem):
    @pl.when(flag[0] == 0)
    def _():
        xb_out[...] = jnp.zeros_like(xb_out)

    @pl.when(flag[0] == 1)
    def _():
        size = g.shape[0]
        copies = [pltpu.make_async_copy(inv.at[1 + i], held.at[i], sem.at[i]) for i in range(2)]
        for copy in copies:
            copy.start()
        for part in range(2):
            assemble((n0, n1, n2, n3), part, 0, size, ae_out.at[part])
        for copy in copies:
            copy.wait()
        near_a, near_e = split(held[0], 1), split(held[1], 1)
        for sweep in range(SWEEPS):
            res = -g[...]
            if sweep:
                x = split(x_out[...], 2)
                left = times_upper_t(split(upper_times([ae_out[0]], x), 2), [ae_out[1]])
                res = res - (left + left.T)
            mid = split(upper_times(near_a, split(res, 1)), 1)
            upd = times_upper_t(mid, near_e)
            upd = 0.25 * (upd + upd.T)
            x_out[...] = x_out[...] + upd if sweep else upd
        xb_out[...] = x_out[...].astype(BF)


def upper_kernel(flag, m0, m1, m2, m3, g_t, inv, x_last, ae_last, xb_out, x, mm, rhs, held, sem):
    @pl.when(flag[0] == 0)
    def _():
        xb_out[...] = jnp.zeros_like(xb_out)

    @pl.when(flag[0] == 1)
    def _():
        size = g_t.shape[0]
        copies = [pltpu.make_async_copy(inv.at[2 * i], held.at[i], sem.at[i]) for i in range(2)]
        for copy in copies:
            copy.start()
        for part in range(2):
            assemble((m0, m1, m2, m3), part, 0, 2 * size, mm.at[part])
        a_last, e_last = ae_last[0], ae_last[1]
        known = split(x_last[...], 2)
        left = sum(dot(mm[0, :, size:], v) for v in known)
        term = times_upper_t(split(left, 2), [e_last])
        left = sum(dot(mm[1, :, size:], v) for v in known)
        term = term + times_upper_t(split(left, 2), [a_last])
        rhs[...] = -g_t[...].T - term
        for copy in copies:
            copy.wait()
        near_a, near_e = split(held[0], 2), split(held[1], 2)
        for sweep in range(SWEEPS):
            res = rhs[...]
            if sweep:
                v = split(x[...], 2)
                left = split(upper_times([mm[0, :, :size]], v), 2)
                term = times_upper_t(left, [e_last])
                left = split(upper_times([mm[1, :, :size]], v), 2)
                term = term + times_upper_t(left, [a_last])
                res = res - term
            mid = split(upper_times(near_a, split(res, 2)), 2)
            upd = 0.5 * times_upper_t(mid, near_e)
            x[...] = x[...] + upd if sweep else upd
        xb_out[...] = x[...].astype(BF)


VMEM = pl.BlockSpec(memory_space=pltpu.VMEM)
SMEM = pl.BlockSpec(memory_space=pltpu.SMEM)
HBM = pl.BlockSpec(memory_space=pl.ANY)
LIMIT = 60 * 1024 * 1024


def solve_last(flag, pieces, g, inverses):
    size = g.shape[0]
    return pl.pallas_call(
        last_kernel,
        out_shape=(
            jax.ShapeDtypeStruct((size, size), F32),
            jax.ShapeDtypeStruct((size, size), BF),
            jax.ShapeDtypeStruct((2, size, size), BF),
        ),
        in_specs=[SMEM] + [VMEM] * 5 + [HBM],
        out_specs=(VMEM,) * 3,
        scratch_shapes=[pltpu.VMEM((2, size, size), F32), pltpu.SemaphoreType.DMA((2,))],
        compiler_params=pltpu.CompilerParams(vmem_limit_bytes=LIMIT),
        cost_estimate=pl.CostEstimate(flops=9 * 10**9, bytes_accessed=8 * 10**6, transcendentals=0),
        name="solve_last",
    )(flag, *pieces, g, inverses)


def solve_upper(flag, pieces, g_t, inverses, x_last, ae_last):
    size = g_t.shape[0]
    return pl.pallas_call(
        upper_kernel,
        out_shape=jax.ShapeDtypeStruct((size, size), BF),
        in_specs=[SMEM] + [VMEM] * 5 + [HBM] + [VMEM] * 2,
        out_specs=VMEM,
        scratch_shapes=[
            pltpu.VMEM((size, size), F32),
            pltpu.VMEM((2, size, 2 * size), BF),
            pltpu.VMEM((size, size), F32),
            pltpu.VMEM((2, size, size), F32),
            pltpu.SemaphoreType.DMA((2,)),
        ],
        compiler_params=pltpu.CompilerParams(vmem_limit_bytes=LIMIT),
        cost_estimate=pl.CostEstimate(flops=12 * 10**9, bytes_accessed=9 * 10**6, transcendentals=0),
        name="solve_upper",
    )(flag, *pieces, g_t, inverses, x_last, ae_last)


def update_kernel(at, *refs):
    row_refs, col_refs = refs[:5], refs[5:13]
    x_own, x_mate, g, out, rows, cols, xs, ye, za, row_sem, col_sem, x_sem = refs[13:]
    size = x_own.shape[0]
    cut = cols.shape[3]
    lanes = g.shape[-1]
    chunks = 2 * size // lanes
    slot = pl.program_id(0)
    k_here = at[7]

    def row_copies(i):
        if i < 3:
            return [pltpu.make_async_copy(row_refs[i], rows.at[i], row_sem.at[i])]
        return [
            pltpu.make_async_copy(row_refs[3 + j], rows.at[3, j], row_sem.at[3 + j])
            for j in range(2)
        ]

    @pl.when(slot == 0)
    def _():
        col_copies = [
            pltpu.make_async_copy(col_refs[i], cols.at[i], col_sem.at[i]) for i in range(8)
        ]
        x_copies = [
            pltpu.make_async_copy(x_own, xs.at[k_here], x_sem.at[0]),
            pltpu.make_async_copy(x_mate, xs.at[1 - k_here], x_sem.at[1]),
        ]
        for copy in x_copies + col_copies + [c for i in range(4) for c in row_copies(i)]:
            copy.start()
        for copy in x_copies:
            copy.wait()

        def piece(p, carry):
            pltpu.make_async_copy(col_refs[0], cols.at[p], col_sem.at[p]).wait()
            row = lax.rem(at[0] + p // 2, 4) * 2 + (at[1] ^ lax.rem(p, 2))
            left = cols[p].reshape(4 * cut, 2 * size)
            low = dot_t(left[:, size:], xs[1]).astype(BF).reshape(2, 2, cut, size)
            high = dot(left[:, :size], xs[1]) + dot(left[:, size:], xs[0])
            high = high.astype(BF).reshape(2, 2, cut, size)
            for b in range(2):
                place = pl.ds(pl.multiple_of(b * size + row * cut, cut), cut)
                za[place, :size] = low[0, b]
                za[place, size:] = high[0, b]
                ye[place, :size] = low[1, b]
                ye[place, size:] = high[1, b]
            return carry

        lax.fori_loop(0, cols.shape[0], piece, 0)

    for i in range(4):

        @pl.when(slot == i)
        def _(i=i):
            for copy in row_copies(i):
                copy.wait()

    wide = 4 * lanes
    step = rows.shape[5]
    tall = 4 * 4 * step
    last = jnp.where(slot == 3, 1, 0)
    third = jnp.where(slot == 2, 1, 0)

    def tile(j, carry):
        place = pl.ds(pl.multiple_of(j * wide, wide), wide)
        acc = dot_t(rows[slot, :, :, 0].reshape(tall, 2 * size), ye[place, :])
        acc = acc + dot_t(rows[slot, :, :, 1].reshape(tall, 2 * size), za[place, :])
        acc = acc.reshape(2, 2, 4, step, wide)
        for dy in range(2):
            yh = at[6] ^ dy ^ (last * k_here)
            for dk in range(2):
                k = k_here ^ dk ^ (third + last * dy)
                for a in range(4):
                    for part in range(4):
                        here = pl.ds(j * 4 + part, step, stride=chunks)
                        value = acc[dy, dk, a, :, part * lanes : (part + 1) * lanes]
                        out[a, 0, yh, k, here, :] = g[a, 0, yh, k, here, :] + value
        return carry

    lax.fori_loop(0, 2 * size // wide, tile, 0)


def update(at, rows, cols, x_own, x_mate, g):
    size = x_own.shape[0]
    block = (4, 1, 2, 2, g.shape[4], g.shape[5])
    spec = pl.BlockSpec(block, lambda i, at: (0, at[2 + i], 0, 0, 0, 0))
    anywhere = pl.BlockSpec(memory_space=pl.ANY)
    return pl.pallas_call(
        update_kernel,
        out_shape=jax.ShapeDtypeStruct(g.shape, F32),
        grid_spec=pltpu.PrefetchScalarGridSpec(
            num_scalar_prefetch=1,
            grid=(4,),
            in_specs=[anywhere] * 15 + [spec],
            out_specs=spec,
            scratch_shapes=[
                pltpu.VMEM((4,) + rows[0].shape, BF),
                pltpu.VMEM((8,) + cols[0].shape, BF),
                pltpu.VMEM((2, size, size), BF),
                pltpu.VMEM((2 * size, 2 * size), BF),
                pltpu.VMEM((2 * size, 2 * size), BF),
                pltpu.SemaphoreType.DMA((5,)),
                pltpu.SemaphoreType.DMA((8,)),
                pltpu.SemaphoreType.DMA((2,)),
            ],
        ),
        compiler_params=pltpu.CompilerParams(
            dimension_semantics=("arbitrary",), vmem_limit_bytes=LIMIT
        ),
        cost_estimate=pl.CostEstimate(
            flops=12 * 10**9, bytes_accessed=30 * 10**6, transcendentals=0
        ),
        name="update",
    )(at, *rows, *cols, x_own, x_mate, g)


def scatter_rule(x, y, z, k):
    yh = x % 2
    near = y % 2 if y // 2 == yh else 1 - y % 2
    return ((x + z) % 4, 2 * yh + near, 2 * k + x // 2, y % 2)


def steps(rhs, panels, inverses):
    row = lax.axis_index("row")
    col = lax.axis_index("col")
    x, yl, z, yh, k = row // 2, row % 2, col // 4, (col // 2) % 2, col % 2
    size = rhs.shape[-1]
    blocks = panels.shape[1]
    local = panels[:, :, 0]
    g_here = rhs[blocks - 1, 0, :, rhs.shape[3] - 1, 0, :]
    flag = jnp.where(row * 16 + col == index(*ROOT), 1, 0).astype(jnp.int32)[None]
    mate_of_root = ROOT[:3] + (0,)

    last_rows = local[:, blocks - 1]
    moved = send(last_rows, lambda x, y, z, k: (x, y + 1, z, k) if x == 3 and y % 2 == 0 else None)
    n_pieces, m_pieces = gather_corner(jnp.concatenate([last_rows[:, :, size:], moved], 2))
    g_t = send(g_here, lambda *at: ROOT if at == mate_of_root else None)
    x_last, x_last_b, ae_last = solve_last(flag, n_pieces, g_here, inverses)
    x_upper_b = solve_upper(flag, m_pieces, g_t, inverses, x_last, ae_last)
    x_last_b = send(x_last_b, lambda *at: mate_of_root if at == ROOT else None)

    mate = send(local, core)
    far = send(local, y_far)
    far_mate = send(far, core)
    own = jnp.stack([jnp.stack([local, mate]), jnp.stack([far, far_mate])])
    side = send(own, z_split)
    across = send(jnp.where(k == 0, own[0], own[1]), z_far)
    rows = [own, side, send(side, core), across, send(across, core)]

    odd = k == 1
    cut = [
        jnp.where(odd, mate[:, 1::2], local[:, 0::2]),
        jnp.where(odd, local[:, 1::2], mate[:, 0::2]),
    ]
    mine = send(jnp.concatenate(cut, 2), scatter_rule)
    near = send(mine, y_near)
    back = [send(mine, x_plus), send(near, x_plus)]
    front = [send(mine, x_minus), send(near, x_minus)]
    opposite = [send(back[0], x_plus), send(front[1], x_minus)]
    cols = [mine, near, *front, *opposite, *back]

    x_own = broadcast(x_upper_b + x_last_b)
    x_mate = send(x_own, core)
    at = jnp.stack(
        [
            (x + 4 - 2 * (z % 2) - yh) % 4,
            yl ^ yh ^ k,
            z,
            jnp.where(odd, z + 1, z + 3) % 4,
            jnp.where(odd, z + 3, z + 1) % 4,
            (z + 2) % 4,
            yh,
            k,
        ]
    ).astype(jnp.int32)
    g = rhs.reshape(4, 4, 2, 2, 256, 128)
    new_rhs = update(at, rows, cols, x_own, x_mate, g).reshape(rhs.shape)

    rows_part = size // 8
    cols_part = size // 16
    window = [
        lax.dynamic_slice(v, (row * rows_part, col * cols_part), (rows_part, cols_part))
        for v in (x_own, x_mate)
    ]
    solved = jnp.stack(
        [jnp.where(odd, window[1], window[0]), jnp.where(odd, window[0], window[1])]
    ).astype(F32)
    return (new_rhs, solved)


def solution(mesh):
    in_specs = (P(None, "row", None, None, "col", None), P(None, None, "row", "col", None), P())
    out_specs = (P(None, "row", None, None, "col", None), P(None, "row", "col"))
    return jax.shard_map(steps, mesh=mesh, in_specs=in_specs, out_specs=out_specs, check_vma=False)
```

```python
import itertools

import jax
import jax.numpy as jnp
from jax import lax
from jax.experimental import pallas as pl
from jax.experimental.pallas import tpu as pltpu
from jax.sharding import PartitionSpec as P


SWEEPS = 3
AXES = ("row", "col")
BF = jnp.bfloat16
F32 = jnp.float32

ROOT = (3, 3, 3, 1)


def index(x, y, z, k):
    return (x * 2 + y % 2) * 16 + z * 4 + (y // 2) * 2 + k


def pairs(rule):
    out = []
    for x, y, z, k in itertools.product(range(4), range(4), range(4), range(2)):
        to = rule(x, y, z, k)
        if to is not None:
            out.append((index(x, y, z, k), index(*to)))
    return out


def send(value, rule):
    return lax.ppermute(value, AXES, pairs(rule))


def x_plus(x, y, z, k):
    return ((x + 1) % 4, y, z, k)


def x_minus(x, y, z, k):
    return ((x - 1) % 4, y, z, k)


def y_far(x, y, z, k):
    return (x, (y + 2) % 4, z, k)


def y_near(x, y, z, k):
    return (x, y ^ 1, z, k)


def core(x, y, z, k):
    return (x, y, z, 1 - k)


def z_split(x, y, z, k):
    return (x, y, (z + (1 if k == 0 else -1)) % 4, k)


def z_far(x, y, z, k):
    return (x, y, (z + 2) % 4, k)


def broadcast(value):
    source = ROOT[:3]
    orders = ((1, 2, 0), (0, 1, 2))
    for step in range(3):
        got = []
        for shift in (2, 1, 3):

            def rule(x, y, z, k, shift=shift):
                at = [x, y, z]
                order = orders[k]
                if any(at[d] != source[d] for d in order[step:]):
                    return None
                at[order[step]] = (at[order[step]] + shift) % 4
                return (*at, k)

            got.append(send(value, rule))
        value = value + got[0] + got[1] + got[2]
    return value


def gather_corner(piece):
    x0, z0 = ROOT[0], ROOT[2]
    got = send(
        piece, lambda x, y, z, k: (x, y, z, 1) if x == x0 and y % 2 == 1 and k == 0 else None
    )
    both = jnp.stack([got, piece])
    far = send(both, lambda x, y, z, k: (x, 3, z, 1) if x == x0 and y == 1 and k == 1 else None)
    four = jnp.stack([far, both])
    size = piece.shape[-1] // 3
    out = []
    for part in (four[..., :size], four[..., size:]):
        pieces = [
            part
            if z1 == z0
            else send(
                part,
                lambda x, y, z, k, z1=z1: ROOT
                if x == x0 and y == 3 and z == z1 and k == 1
                else None,
            )
            for z1 in range(4)
        ]
        out.append(pieces)
    return out


def dot(left, right):
    return jnp.dot(left, right, preferred_element_type=F32)


def dot_t(left, right):
    return lax.dot_general(left, right, (((1,), (1,)), ((), ())), preferred_element_type=F32)


def split(value, count):
    high = value.astype(BF)
    if count == 1:
        return [high]
    return [high, (value - high.astype(F32)).astype(BF)]


def terms(left, right):
    depth = max(len(left), len(right))
    return [(i, j) for i in range(len(left)) for j in range(len(right)) if i + j < depth]


def upper_times(upper, value):
    half = value[0].shape[0] // 2
    top = sum(dot(upper[i][:half, :], value[j]) for i, j in terms(upper, value))
    low = sum(dot(upper[i][half:, half:], value[j][half:, :]) for i, j in terms(upper, value))
    return jnp.concatenate([top, low], 0)


def times_upper_t(value, upper):
    half = value[0].shape[1] // 2
    left = sum(dot_t(value[i], upper[j][:half, :]) for i, j in terms(value, upper))
    right = sum(dot_t(value[i][:, half:], upper[j][half:, half:]) for i, j in terms(value, upper))
    return jnp.concatenate([left, right], 1)


def assemble(refs, part, lo, hi, out):
    step = refs[0].shape[3]
    at = 0
    for ref in refs:
        for yh in range(2):
            for k in range(2):
                out[at : at + step, :] = ref[yh, k, part, :, lo:hi]
                at += step


def last_kernel(flag, n0, n1, n2, n3, g, inv, x_out, xb_out, ae_out, held, sem):
    @pl.when(flag[0] == 0)
    def _():
        xb_out[...] = jnp.zeros_like(xb_out)

    @pl.when(flag[0] == 1)
    def _():
        size = g.shape[0]
        copies = [pltpu.make_async_copy(inv.at[1 + i], held.at[i], sem.at[i]) for i in range(2)]
        for copy in copies:
            copy.start()
        for part in range(2):
            assemble((n0, n1, n2, n3), part, 0, size, ae_out.at[part])
        for copy in copies:
            copy.wait()
        near_a, near_e = split(held[0], 1), split(held[1], 1)
        for sweep in range(SWEEPS):
            res = -g[...]
            if sweep:
                x = split(x_out[...], 2)
                left = times_upper_t(split(upper_times([ae_out[0]], x), 2), [ae_out[1]])
                res = res - (left + left.T)
            mid = split(upper_times(near_a, split(res, 1)), 1)
            upd = times_upper_t(mid, near_e)
            upd = 0.25 * (upd + upd.T)
            x_out[...] = x_out[...] + upd if sweep else upd
        xb_out[...] = x_out[...].astype(BF)


def upper_kernel(flag, m0, m1, m2, m3, g_t, inv, x_last, ae_last, passed, xb_out, x, mm, rhs, held, sem):
    @pl.when(flag[0] == 0)
    def _():
        xb_out[...] = passed[...]

    @pl.when(flag[0] == 1)
    def _():
        size = g_t.shape[0]
        copies = [pltpu.make_async_copy(inv.at[2 * i], held.at[i], sem.at[i]) for i in range(2)]
        for copy in copies:
            copy.start()
        for part in range(2):
            assemble((m0, m1, m2, m3), part, 0, 2 * size, mm.at[part])
        a_last, e_last = ae_last[0], ae_last[1]
        known = split(x_last[...], 2)
        left = sum(dot(mm[0, :, size:], v) for v in known)
        term = times_upper_t(split(left, 2), [e_last])
        left = sum(dot(mm[1, :, size:], v) for v in known)
        term = term + times_upper_t(split(left, 2), [a_last])
        rhs[...] = -g_t[...].T - term
        for copy in copies:
            copy.wait()
        near_a, near_e = split(held[0], 2), split(held[1], 2)
        for sweep in range(SWEEPS):
            res = rhs[...]
            if sweep:
                v = split(x[...], 2)
                left = split(upper_times([mm[0, :, :size]], v), 2)
                term = times_upper_t(left, [e_last])
                left = split(upper_times([mm[1, :, :size]], v), 2)
                term = term + times_upper_t(left, [a_last])
                res = res - term
            mid = split(upper_times(near_a, split(res, 2)), 2)
            upd = 0.5 * times_upper_t(mid, near_e)
            x[...] = x[...] + upd if sweep else upd
        xb_out[...] = x[...].astype(BF)


VMEM = pl.BlockSpec(memory_space=pltpu.VMEM)
SMEM = pl.BlockSpec(memory_space=pltpu.SMEM)
HBM = pl.BlockSpec(memory_space=pl.ANY)
LIMIT = 60 * 1024 * 1024


def solve_last(flag, pieces, g, inverses):
    size = g.shape[0]
    return pl.pallas_call(
        last_kernel,
        out_shape=(
            jax.ShapeDtypeStruct((size, size), F32),
            jax.ShapeDtypeStruct((size, size), BF),
            jax.ShapeDtypeStruct((2, size, size), BF),
        ),
        in_specs=[SMEM] + [VMEM] * 5 + [HBM],
        out_specs=(VMEM,) * 3,
        scratch_shapes=[pltpu.VMEM((2, size, size), F32), pltpu.SemaphoreType.DMA((2,))],
        compiler_params=pltpu.CompilerParams(vmem_limit_bytes=LIMIT),
        cost_estimate=pl.CostEstimate(flops=9 * 10**9, bytes_accessed=8 * 10**6, transcendentals=0),
        name="solve_last",
    )(flag, *pieces, g, inverses)


def solve_upper(flag, pieces, g_t, inverses, x_last, ae_last, passed):
    size = g_t.shape[0]
    return pl.pallas_call(
        upper_kernel,
        out_shape=jax.ShapeDtypeStruct((size, size), BF),
        in_specs=[SMEM] + [VMEM] * 5 + [HBM] + [VMEM] * 3,
        out_specs=VMEM,
        scratch_shapes=[
            pltpu.VMEM((size, size), F32),
            pltpu.VMEM((2, size, 2 * size), BF),
            pltpu.VMEM((size, size), F32),
            pltpu.VMEM((2, size, size), F32),
            pltpu.SemaphoreType.DMA((2,)),
        ],
        compiler_params=pltpu.CompilerParams(vmem_limit_bytes=LIMIT),
        cost_estimate=pl.CostEstimate(flops=12 * 10**9, bytes_accessed=9 * 10**6, transcendentals=0),
        name="solve_upper",
    )(flag, *pieces, g_t, inverses, x_last, ae_last, passed)


def update_kernel(at, *refs):
    row_refs, col_refs = refs[:5], refs[5:13]
    x_own, x_mate, g, out, rows, cols, xs, ye, za, row_sem, col_sem, x_sem = refs[13:]
    size = x_own.shape[0]
    cut = cols.shape[3]
    lanes = g.shape[-1]
    chunks = 2 * size // lanes
    slot = pl.program_id(0)
    k_here = at[7]

    def row_copies(i):
        if i < 3:
            return [pltpu.make_async_copy(row_refs[i], rows.at[i], row_sem.at[i])]
        return [
            pltpu.make_async_copy(row_refs[3 + j], rows.at[3, j], row_sem.at[3 + j])
            for j in range(2)
        ]

    @pl.when(slot == 0)
    def _():
        col_copies = [
            pltpu.make_async_copy(col_refs[i], cols.at[i], col_sem.at[i]) for i in range(8)
        ]
        x_copies = [
            pltpu.make_async_copy(x_own, xs.at[k_here], x_sem.at[0]),
            pltpu.make_async_copy(x_mate, xs.at[1 - k_here], x_sem.at[1]),
        ]
        for copy in x_copies + col_copies + [c for i in range(4) for c in row_copies(i)]:
            copy.start()
        for copy in x_copies:
            copy.wait()

        def piece(p, carry):
            pltpu.make_async_copy(col_refs[0], cols.at[p], col_sem.at[p]).wait()
            row = lax.rem(at[0] + p // 2, 4) * 2 + (at[1] ^ lax.rem(p, 2))
            left = cols[p].reshape(4 * cut, 2 * size)
            low = dot_t(left[:, size:], xs[1]).astype(BF).reshape(2, 2, cut, size)
            high = dot(left[:, :size], xs[1]) + dot(left[:, size:], xs[0])
            high = high.astype(BF).reshape(2, 2, cut, size)
            for b in range(2):
                place = pl.ds(pl.multiple_of(b * size + row * cut, cut), cut)
                za[place, :size] = low[0, b]
                za[place, size:] = high[0, b]
                ye[place, :size] = low[1, b]
                ye[place, size:] = high[1, b]
            return carry

        lax.fori_loop(0, cols.shape[0], piece, 0)

    for i in range(4):

        @pl.when(slot == i)
        def _(i=i):
            for copy in row_copies(i):
                copy.wait()

    wide = 4 * lanes
    step = rows.shape[5]
    tall = 4 * 4 * step
    last = jnp.where(slot == 3, 1, 0)
    third = jnp.where(slot == 2, 1, 0)

    def tile(j, carry):
        place = pl.ds(pl.multiple_of(j * wide, wide), wide)
        acc = dot_t(rows[slot, :, :, 0].reshape(tall, 2 * size), ye[place, :])
        acc = acc + dot_t(rows[slot, :, :, 1].reshape(tall, 2 * size), za[place, :])
        acc = acc.reshape(2, 2, 4, step, wide)
        for dy in range(2):
            yh = at[6] ^ dy ^ (last * k_here)
            for dk in range(2):
                k = k_here ^ dk ^ (third + last * dy)
                for a in range(4):
                    for part in range(4):
                        here = pl.ds(j * 4 + part, step, stride=chunks)
                        value = acc[dy, dk, a, :, part * lanes : (part + 1) * lanes]
                        out[a, 0, yh, k, here, :] = g[a, 0, yh, k, here, :] + value
        return carry

    lax.fori_loop(0, 2 * size // wide, tile, 0)


def update(at, rows, cols, x_own, x_mate, g):
    size = x_own.shape[0]
    block = (4, 1, 2, 2, g.shape[4], g.shape[5])
    spec = pl.BlockSpec(block, lambda i, at: (0, at[2 + i], 0, 0, 0, 0))
    anywhere = pl.BlockSpec(memory_space=pl.ANY)
    return pl.pallas_call(
        update_kernel,
        out_shape=jax.ShapeDtypeStruct(g.shape, F32),
        grid_spec=pltpu.PrefetchScalarGridSpec(
            num_scalar_prefetch=1,
            grid=(4,),
            in_specs=[anywhere] * 15 + [spec],
            out_specs=spec,
            scratch_shapes=[
                pltpu.VMEM((4,) + rows[0].shape, BF),
                pltpu.VMEM((8,) + cols[0].shape, BF),
                pltpu.VMEM((2, size, size), BF),
                pltpu.VMEM((2 * size, 2 * size), BF),
                pltpu.VMEM((2 * size, 2 * size), BF),
                pltpu.SemaphoreType.DMA((5,)),
                pltpu.SemaphoreType.DMA((8,)),
                pltpu.SemaphoreType.DMA((2,)),
            ],
        ),
        compiler_params=pltpu.CompilerParams(
            dimension_semantics=("arbitrary",), vmem_limit_bytes=LIMIT
        ),
        cost_estimate=pl.CostEstimate(
            flops=12 * 10**9, bytes_accessed=30 * 10**6, transcendentals=0
        ),
        name="update",
    )(at, *rows, *cols, x_own, x_mate, g)


def scatter_rule(x, y, z, k):
    yh = x % 2
    near = y % 2 if y // 2 == yh else 1 - y % 2
    return ((x + z) % 4, 2 * yh + near, 2 * k + x // 2, y % 2)


def steps(rhs, panels, inverses):
    row = lax.axis_index("row")
    col = lax.axis_index("col")
    x, yl, z, yh, k = row // 2, row % 2, col // 4, (col // 2) % 2, col % 2
    size = rhs.shape[-1]
    blocks = panels.shape[1]
    local = panels[:, :, 0]
    g_here = rhs[blocks - 1, 0, :, rhs.shape[3] - 1, 0, :]
    flag = jnp.where(row * 16 + col == index(*ROOT), 1, 0).astype(jnp.int32)[None]
    mate_of_root = ROOT[:3] + (0,)

    last_rows = local[:, blocks - 1]
    moved = send(last_rows, lambda x, y, z, k: (x, y + 1, z, k) if x == 3 and y % 2 == 0 else None)
    n_pieces, m_pieces = gather_corner(jnp.concatenate([last_rows[:, :, size:], moved], 2))
    g_t = send(g_here, lambda *at: ROOT if at == mate_of_root else None)
    x_last, x_last_b, ae_last = solve_last(flag, n_pieces, g_here, inverses)
    passed = send(x_last_b, lambda *at: mate_of_root if at == ROOT else None)
    x_first = solve_upper(flag, m_pieces, g_t, inverses, x_last, ae_last, passed)

    mate = send(local, core)
    far = send(local, y_far)
    far_mate = send(far, core)
    own = jnp.stack([jnp.stack([local, mate]), jnp.stack([far, far_mate])])
    side = send(own, z_split)
    across = send(jnp.where(k == 0, own[0], own[1]), z_far)
    rows = [own, side, send(side, core), across, send(across, core)]

    odd = k == 1
    cut = [
        jnp.where(odd, mate[:, 1::2], local[:, 0::2]),
        jnp.where(odd, local[:, 1::2], mate[:, 0::2]),
    ]
    mine = send(jnp.concatenate(cut, 2), scatter_rule)
    near = send(mine, y_near)
    back = [send(mine, x_plus), send(near, x_plus)]
    front = [send(mine, x_minus), send(near, x_minus)]
    opposite = [send(back[0], x_plus), send(front[1], x_minus)]
    cols = [mine, near, *front, *opposite, *back]

    x_own = broadcast(x_first)
    x_mate = send(x_own, core)
    at = jnp.stack(
        [
            (x + 4 - 2 * (z % 2) - yh) % 4,
            yl ^ yh ^ k,
            z,
            jnp.where(odd, z + 1, z + 3) % 4,
            jnp.where(odd, z + 3, z + 1) % 4,
            (z + 2) % 4,
            yh,
            k,
        ]
    ).astype(jnp.int32)
    g = rhs.reshape(4, 4, 2, 2, 256, 128)
    new_rhs = update(at, rows, cols, x_own, x_mate, g).reshape(rhs.shape)

    rows_part = size // 8
    cols_part = size // 16
    window = [
        lax.dynamic_slice(v, (row * rows_part, col * cols_part), (rows_part, cols_part))
        for v in (x_own, x_mate)
    ]
    solved = jnp.stack(
        [jnp.where(odd, window[1], window[0]), jnp.where(odd, window[0], window[1])]
    ).astype(F32)
    return (new_rhs, solved)


def solution(mesh):
    in_specs = (P(None, "row", None, None, "col", None), P(None, None, "row", "col", None), P())
    out_specs = (P(None, "row", None, None, "col", None), P(None, "row", "col"))
    return jax.shard_map(steps, mesh=mesh, in_specs=in_specs, out_specs=out_specs, check_vma=False)
```
